32 devices in a mesh: dp: 4 (over x, core), expert: 8 (over z, y).
Axes of the slice: x: 2, y: 2, z: 4, core: 2. Of those that a mesh axis runs over, the one named last changes fastest.
Arguments:
- tokens: bfloat16 [4096, 2048], P(('dp', 'expert')), may hold values from -6 to 6
- expert_ids: int32 [4096, 8], P(('dp', 'expert')), may hold values from 0 to 127, all different within a row; in each aligned block of 128 rows (0 to 127, 128 to 255, ...) at most 20 rows name the same one
- gate_probs: float32 [4096, 8], P(('dp', 'expert')), may hold values from 0.05 to 1
- gate_weight: bfloat16 [128, 768, 2048], P(('dp', 'expert')), may hold values from -0.125 to 0.125
- up_weight: bfloat16 [128, 768, 2048], P(('dp', 'expert')), may hold values from -0.125 to 0.125
- down_weight: bfloat16 [128, 768, 2048], P(('dp', 'expert')), may hold values from -0.4375 to 0.4375
Outputs:
- mixed: bfloat16 [4096, 2048], P(('dp', 'expert'))
- expert_load: float32 [128], replicated
The draws below stay inside these ranges and needn't reach their ends.
Inputs may be any that keep to these rules, and one draw needn't show every extreme that they name: `expert_ids`: in each block of 128 consecutive tokens no expert is named by more than 20 pairs, a bound that some blocks reach; every expert is named somewhere.
All inputs are finite; a program needn't handle non-finite values.
Results may differ from the reference program's by a relative error of at most 0.0085.
Values may be sent and summed in bfloat16 or wider, within the bound.
A program may use at most 128 MiB of HBM per device.

```python
import math
import jax
import jax.numpy as jnp
import numpy as np
from jax import lax

D = 2048
FF = 768
EXPERTS = 128
TOP = 8
TOK_DEV = 128
CAP = 20
TOKENS = 4096
DEVICES = 32


def shard_levels(stream_key, extent, split, low, top_value):
    def one(position, shards_of):
        draws = jax.random.uniform(jax.random.fold_in(jax.random.fold_in(stream_key, 6), position), (shards_of,), jnp.float32, low / len(split), top_value / len(split))
        return jnp.repeat(jnp.exp(draws), extent[position] // shards_of).reshape((-1,) + (1,) * (len(extent) - position - 1))

    level = one(*split[0])
    for cut in split[1:]:
        level = level * one(*cut)
    return level


def shared_out(stream_key, own, number, rows, amount, top, most, lean):
    sequence = jax.random.permutation(stream_key, amount)
    packed, ordinary = portions_of(amount, rows * top, most, lean, True), portions_of(amount, rows * top, most, lean, False)
    places = jnp.arange(amount)

    def named(sizes, rotation):
        used = int((sizes > 0).sum())
        fixed = max(1, used // 4)
        shifted = fixed + (places - fixed + rotation * (used - fixed)) % max(1, amount - fixed)
        return jnp.zeros((amount,), jnp.int32).at[sequence[jnp.where(places < fixed, places, shifted)]].set(jnp.asarray(sizes, jnp.int32))

    sizes = jnp.where(number % 4 == 0, named(packed, number // 4), named(ordinary, number - number // 4 - 1))
    mixed = jax.random.permutation(jax.random.fold_in(own, 3), amount)
    giver, sink = mixed[0:amount // 2 * 2:2], mixed[1:amount // 2 * 2:2]
    margin = jnp.minimum(sizes[giver] - 1, most - sizes[sink]) // 2
    margin = jnp.where((giver == sequence[0]) | (sink == sequence[0]) | (sizes[sink] == 0), 0, jnp.maximum(margin, 0))
    shifted = jax.random.randint(jax.random.fold_in(own, 4), (amount // 2,), 0, 1 << 20) % (margin + 1)
    sizes = sizes.at[giver].add(-shifted).at[sink].add(shifted)
    labels = jnp.searchsorted(jnp.cumsum(sizes), jnp.arange(rows * top), side="right").astype(jnp.int32)
    grid = labels.reshape(top, rows).T
    grid = grid[jax.random.permutation(jax.random.fold_in(own, 1), rows)]
    rotation = jax.random.randint(jax.random.fold_in(own, 2), (rows, 1), 0, top)
    return jnp.take_along_axis(grid, (jnp.arange(top)[None, :] + rotation) % top, axis=1)


def portions_of(number_of, total, reach, skew, full):
    weights = [(1 << 20) // math.isqrt(grade ** skew) + 1 for grade in range(1, number_of + 1)]
    largest = reach if full else min(reach, max(-(-total // number_of), total * weights[0] // sum(weights)))
    least = 1 if total - largest >= number_of - 1 else 0
    holding, spare = [largest] + [least] * (number_of - 1), total - largest - least * (number_of - 1)
    while spare > 0:
        candidates = [i for i in range(1, number_of) if holding[i] < largest] or [i for i in range(1, number_of) if holding[i] < reach]
        whole, remaining = sum([weights[i] for i in candidates]), spare
        for i in candidates:
            more = min(reach - holding[i], max(1, remaining * weights[i] // whole), spare)
            holding[i] = holding[i] + more
            spare = spare - more
    return np.array(holding)


def scatter_about(own_key, extent, spread, most, split=(), kind=jnp.bfloat16):
    result = spread * jax.random.normal(own_key, extent, jnp.float32)
    if split:
        result = result * shard_levels(own_key, extent, split, -0.22, 0.18)
    return jnp.clip(result, -most, most).astype(kind)


def setup_inputs(seed: int = 0) -> dict:
    arg_keys = jax.random.split(jax.random.key(seed), 7)
    tokens = scatter_about(arg_keys[0], (TOKENS, D), 1.0, 6.0, ((0, 32),))
    expert_ids_keys = jax.random.split(jax.random.fold_in(arg_keys[1], 1), TOKENS // TOK_DEV)
    expert_ids_turns = jax.random.permutation(jax.random.fold_in(arg_keys[1], 3), TOKENS // TOK_DEV)
    expert_ids = jax.vmap(lambda own, number: shared_out(jax.random.fold_in(arg_keys[1], 2), own, number, TOK_DEV, EXPERTS, TOP, CAP, 2))(expert_ids_keys, expert_ids_turns).reshape((TOKENS, TOP))
    gate_probs = jnp.clip(jnp.exp(math.log(1.0) - 2.9957323 * jax.random.uniform(arg_keys[2], (TOKENS, TOP), jnp.float32) ** shard_levels(arg_keys[2], (TOKENS, TOP), ((0, 32),), -0.2, 0.2)), 0.05, 1.0)
    gate_weight = scatter_about(arg_keys[3], (EXPERTS, FF, D), D ** -0.5, 0.125, ((0, 32),))
    up_weight = scatter_about(arg_keys[4], (EXPERTS, FF, D), D ** -0.5, 0.125, ((0, 32),))
    down_weight = scatter_about(arg_keys[5], (EXPERTS, FF, D), (FF // 4) ** -0.5, 0.4375, ((0, 32),))
    return {"tokens": tokens, "expert_ids": expert_ids, "gate_probs": gate_probs, "gate_weight": gate_weight, "up_weight": up_weight, "down_weight": down_weight}


def expert_rows(row_block, gate_matrix, up_matrix, down_matrix):
    gate_part = jnp.dot(row_block, gate_matrix.T, preferred_element_type=jnp.float32)
    up_part = jnp.dot(row_block, up_matrix.T, preferred_element_type=jnp.float32)
    hidden = (jax.nn.silu(gate_part) * up_part).astype(jnp.bfloat16)
    return jnp.dot(hidden, down_matrix, preferred_element_type=jnp.float32).astype(jnp.bfloat16)


def slot_targets(block):
    one_hot = (block[:, None] == jnp.arange(EXPERTS, dtype=jnp.int32)[None, :]).astype(jnp.int32)
    earlier = jnp.cumsum(one_hot, axis=0) - one_hot
    return (block * CAP + jnp.sum(earlier * one_hot, axis=1)).astype(jnp.int32)


def reference(tokens, expert_ids, gate_probs, gate_weight, up_weight, down_weight):
    weights = gate_probs / jnp.sum(gate_probs, axis=1, keepdims=True)
    blocks = expert_ids.reshape(DEVICES, TOK_DEV * TOP)
    target = lax.map(slot_targets, blocks)
    device_of = jnp.arange(DEVICES, dtype=jnp.int32)[:, None]
    pair_of = jnp.arange(TOK_DEV * TOP, dtype=jnp.int32)[None, :]
    place = (target // CAP) * (DEVICES * CAP) + device_of * CAP + target % CAP
    row_of = device_of * TOK_DEV + pair_of // TOP
    table = jnp.full((EXPERTS * DEVICES * CAP,), TOKENS, jnp.int32)
    table = table.at[place.reshape(-1)].set(row_of.reshape(-1)).reshape(EXPERTS, DEVICES * CAP)
    shares = jnp.zeros((EXPERTS * DEVICES * CAP,), jnp.float32)
    shares = shares.at[place.reshape(-1)].set(weights.reshape(-1)).reshape(EXPERTS, DEVICES * CAP)
    padded = jnp.concatenate([tokens, jnp.zeros((1, D), tokens.dtype)], axis=0)

    def visit(total, inputs):
        row_ids, share_row, gate_matrix, up_matrix, down_matrix = inputs
        produced = expert_rows(padded[row_ids], gate_matrix, up_matrix, down_matrix)
        return total.at[row_ids].add(share_row[:, None] * produced.astype(jnp.float32)), None

    total, unused = lax.scan(visit, jnp.zeros((TOKENS + 1, D), jnp.float32),
                             (table, shares, gate_weight, up_weight, down_weight))
    mixed = total[:TOKENS].astype(jnp.bfloat16)
    counts = jnp.zeros((EXPERTS,), jnp.float32).at[expert_ids.reshape(-1)].add(1.0)
    expert_load = counts * (EXPERTS / (TOKENS * TOP))
    return mixed, expert_load
```

```python
import jax
import jax.numpy as jnp
from jax import lax
from jax.sharding import PartitionSpec as P

CAP = 20
AXES = ("dp", "expert")
CHUNKS = 2


def on_device(tokens, expert_ids, gate_probs, gate_weight, up_weight, down_weight):
    rows, features = tokens.shape
    top = expert_ids.shape[1]
    owned = gate_weight.shape[0]
    devices = lax.axis_size(AXES)
    me = lax.axis_index(AXES)
    experts = owned * devices
    bf16, f32 = jnp.bfloat16, jnp.float32
    cut = features // CHUNKS

    weights = gate_probs / jnp.sum(gate_probs, axis=1, keepdims=True)
    every = lax.iota(jnp.int32, experts)
    named = (expert_ids.reshape(rows * top)[:, None] == every[None, :]).astype(f32)
    counts = jnp.sum(named, axis=0)
    meta = jnp.concatenate(
        [expert_ids.astype(f32).reshape(-1), weights.reshape(-1), counts]
    )
    meta = lax.all_gather(meta.reshape(1, -1), AXES, axis=0, tiled=True)
    arriving = [
        lax.all_gather(tokens[:, c * cut : (c + 1) * cut], AXES, axis=0, tiled=True)
        for c in range(CHUNKS)
    ]
    pairs = rows * top
    ids_all = meta[:, :pairs].reshape(devices, rows, top).astype(jnp.int32)
    w_all = meta[:, pairs : 2 * pairs].reshape(devices, rows, top)
    expert_load = jnp.sum(meta[:, 2 * pairs :], axis=0) * (experts / (rows * devices * top))

    mine = me * owned + lax.iota(jnp.int32, owned)
    hit = (ids_all[:, None, :, :] == mine[None, :, None, None]).astype(f32)
    chosen = jnp.sum(hit, axis=3)
    share = jnp.sum(hit * w_all[:, None, :, :], axis=3)
    before = (lax.iota(jnp.int32, rows)[:, None] < lax.iota(jnp.int32, rows)[None, :]).astype(bf16)
    slot = jnp.einsum("bet,tu->beu", chosen.astype(bf16), before, preferred_element_type=f32)
    slot = jnp.where(chosen > 0, slot, -1.0)
    pick = slot[:, :, None, :] == lax.iota(jnp.int32, CAP).astype(f32)[None, None, :, None]
    scale = jnp.sum(jnp.where(pick, share[:, :, None, :], 0.0), axis=3)
    pick = pick.astype(bf16)

    gate = up = 0.0
    for c in range(CHUNKS):
        block = arriving[c].reshape(devices, rows, cut)
        x = jnp.einsum("best,btd->ebsd", pick, block, preferred_element_type=f32)
        x = x.astype(bf16).reshape(owned, devices * CAP, cut)
        span = slice(c * cut, (c + 1) * cut)
        gate += jnp.einsum("ekd,efd->ekf", x, gate_weight[:, :, span], preferred_element_type=f32)
        up += jnp.einsum("ekd,efd->ekf", x, up_weight[:, :, span], preferred_element_type=f32)
    hidden = (jax.nn.silu(gate) * up).astype(bf16)
    scale = scale.transpose(1, 0, 2).reshape(owned, devices * CAP, 1)
    mixed = []
    for c in range(CHUNKS):
        span = slice(c * cut, (c + 1) * cut)
        y = jnp.einsum("ekf,efd->ekd", hidden, down_weight[:, :, span], preferred_element_type=f32)
        y = (y * scale).astype(bf16).reshape(owned, devices, CAP, cut)
        part = jnp.einsum("best,ebsd->btd", pick, y, preferred_element_type=f32)
        part = part.astype(bf16).reshape(devices * rows, cut)
        mixed.append(lax.psum_scatter(part, AXES, scatter_dimension=0, tiled=True))
    return jnp.concatenate(mixed, axis=1), expert_load


def solution(mesh):
    in_specs = (
        P(AXES, None),
        P(AXES, None),
        P(AXES, None),
        P(AXES, None, None),
        P(AXES, None, None),
        P(AXES, None, None),
    )
    return jax.shard_map(
        on_device, mesh=mesh, in_specs=in_specs, out_specs=(P(AXES, None), P()), check_vma=False
    )
```

```python
import jax
import jax.numpy as jnp
from jax import lax
from jax.sharding import PartitionSpec as P

CAP = 20
AXES = ("dp", "expert")


def on_device(tokens, expert_ids, gate_probs, gate_weight, up_weight, down_weight):
    rows, features = tokens.shape
    top = expert_ids.shape[1]
    owned = gate_weight.shape[0]
    devices = lax.axis_size(AXES)
    me = lax.axis_index(AXES)
    experts = owned * devices
    bf16, f32 = jnp.bfloat16, jnp.float32

    pair = lax.axis_size("expert")
    bits = [1 << i for i in range(devices.bit_length() - 1) if (1 << i) != pair]
    depth = len(bits)
    others = 1 << depth
    orders = [bits[i:] + bits[:i] for i in (depth - 1, 0, 1)]
    step = features // 8
    bounds = [0, 3 * step, 6 * step, features]
    spans = [slice(bounds[i], bounds[i + 1]) for i in range(3)]

    def swap(value, bit):
        return lax.ppermute(value, AXES, [(i, i ^ bit) for i in range(devices)])

    def spread(value, order):
        value = value.reshape((1,) * depth + value.shape)
        for bit in reversed(order):
            axis = depth - 1 - bits.index(bit)
            value = jnp.concatenate([value, swap(value, bit)], axis=axis)
        return value

    def collect(value, order):
        for bit in order:
            axis = depth - 1 - bits.index(bit)
            far = lax.slice_in_dim(value, 1, 2, axis=axis)
            near = lax.slice_in_dim(value, 0, 1, axis=axis)
            value = (near.astype(f32) + swap(far, bit).astype(f32)).astype(bf16)
        return value.reshape(value.shape[depth:])

    weights = gate_probs / jnp.sum(gate_probs, axis=1, keepdims=True)
    every = lax.iota(jnp.int32, experts)
    named = (expert_ids.reshape(rows * top)[:, None] == every[None, :]).astype(f32)
    meta = jnp.concatenate(
        [expert_ids.astype(f32).reshape(-1), weights.reshape(-1), jnp.sum(named, axis=0)]
    ).reshape(1, -1)
    meta = spread(meta, orders[1])
    meta = jnp.stack([meta, swap(meta, pair)]).reshape(2, others, -1)
    near = [spread(tokens[:, spans[p]], orders[p]) for p in range(3)]
    far = [swap(near[p], pair) for p in range(3)]
    arrived = [
        [v.reshape(others, rows, v.shape[-1]) for v in near],
        [v.reshape(others, rows, v.shape[-1]) for v in far],
    ]

    pairs = rows * top
    expert_load = jnp.sum(meta[:, :, 2 * pairs :], axis=(0, 1)) * (
        experts / (rows * devices * top)
    )
    mine = me * owned + lax.iota(jnp.int32, owned)
    before = (lax.iota(jnp.int32, rows)[:, None] < lax.iota(jnp.int32, rows)[None, :]).astype(bf16)

    def apply(half):
        ids_all = meta[half, :, :pairs].reshape(others, rows, top).astype(jnp.int32)
        w_all = meta[half, :, pairs : 2 * pairs].reshape(others, rows, top)
        hit = (ids_all[:, None, :, :] == mine[None, :, None, None]).astype(f32)
        chosen = jnp.sum(hit, axis=3)
        share = jnp.sum(hit * w_all[:, None, :, :], axis=3)
        slot = jnp.einsum("bet,tu->beu", chosen.astype(bf16), before, preferred_element_type=f32)
        slot = jnp.where(chosen > 0, slot, -1.0)
        pick = slot[:, :, None, :] == lax.iota(jnp.int32, CAP).astype(f32)[None, None, :, None]
        scale = jnp.sum(jnp.where(pick, share[:, :, None, :], 0.0), axis=3)
        pick = pick.astype(bf16)
        gate = up = 0.0
        for p in range(3):
            x = jnp.einsum("best,btd->ebsd", pick, arrived[half][p], preferred_element_type=f32)
            x = x.astype(bf16).reshape(owned, others * CAP, -1)
            gate += jnp.einsum(
                "ekd,efd->ekf", x, gate_weight[:, :, spans[p]], preferred_element_type=f32
            )
            up += jnp.einsum(
                "ekd,efd->ekf", x, up_weight[:, :, spans[p]], preferred_element_type=f32
            )
        hidden = (jax.nn.silu(gate) * up).astype(bf16)
        scale = scale.transpose(1, 0, 2).reshape(owned, others * CAP, 1)
        parts = []
        for p in range(3):
            y = jnp.einsum(
                "ekf,efd->ekd", hidden, down_weight[:, :, spans[p]], preferred_element_type=f32
            )
            y = (y * scale).astype(bf16).reshape(owned, others, CAP, -1)
            part = jnp.einsum("best,ebsd->btd", pick, y, preferred_element_type=f32)
            parts.append(part.astype(bf16).reshape((2,) * depth + (rows, -1)))
        return parts

    kept = apply(0)
    given = apply(1)
    mixed = []
    for p in range(3):
        total = (kept[p].astype(f32) + swap(given[p], pair).astype(f32)).astype(bf16)
        mixed.append(collect(total, orders[p]))
    return jnp.concatenate(mixed, axis=1), expert_load


def solution(mesh):
    in_specs = (
        P(AXES, None),
        P(AXES, None),
        P(AXES, None),
        P(AXES, None, None),
        P(AXES, None, None),
        P(AXES, None, None),
    )
    return jax.shard_map(
        on_device, mesh=mesh, in_specs=in_specs, out_specs=(P(AXES, None), P()), check_vma=False
    )
```

```python
import jax
import jax.numpy as jnp
from jax import lax
from jax.sharding import PartitionSpec as P

CAP = 20
AXES = ("dp", "expert")


def on_device(tokens, expert_ids, gate_probs, gate_weight, up_weight, down_weight):
    rows, features = tokens.shape
    top = expert_ids.shape[1]
    owned = gate_weight.shape[0]
    devices = lax.axis_size(AXES)
    me = lax.axis_index(AXES)
    experts = owned * devices
    bf16, f32 = jnp.bfloat16, jnp.float32

    pair = lax.axis_size("expert")
    bits = [1 << i for i in range(devices.bit_length() - 1) if (1 << i) != pair]
    depth = len(bits)
    others = 1 << depth
    orders = [bits[i:] + bits[:i] for i in (depth - 1, 0, 1)]
    step = features // 8
    bounds = [0, 3 * step, 6 * step, features]
    spans = [slice(bounds[i], bounds[i + 1]) for i in range(3)]

    def swap(value, bit):
        return lax.ppermute(value, AXES, [(i, i ^ bit) for i in range(devices)])

    def spread(value, order):
        value = value.reshape((1,) * depth + value.shape)
        for bit in reversed(order):
            axis = depth - 1 - bits.index(bit)
            value = jnp.concatenate([value, swap(value, bit)], axis=axis)
        return value

    def collect(value, order):
        for bit in order:
            axis = depth - 1 - bits.index(bit)
            far = lax.slice_in_dim(value, 1, 2, axis=axis)
            near = lax.slice_in_dim(value, 0, 1, axis=axis)
            value = (near.astype(f32) + swap(far, bit).astype(f32)).astype(bf16)
        return value.reshape(value.shape[depth:])

    weights = gate_probs / jnp.sum(gate_probs, axis=1, keepdims=True)
    every = lax.iota(jnp.int32, experts)
    named = (expert_ids.reshape(rows * top)[:, None] == every[None, :]).astype(f32)
    meta = jnp.concatenate(
        [expert_ids.astype(f32).reshape(-1), weights.reshape(-1), jnp.sum(named, axis=0)]
    ).reshape(1, -1)
    meta = spread(meta, orders[1])
    meta = jnp.stack([meta, swap(meta, pair)]).reshape(2, others, -1)
    near = [spread(tokens[:, spans[p]], orders[p]) for p in range(3)]
    far = [swap(near[p], pair) for p in range(3)]
    arrived = [
        [v.reshape(others, rows, v.shape[-1]) for v in near],
        [v.reshape(others, rows, v.shape[-1]) for v in far],
    ]

    pairs = rows * top
    expert_load = jnp.sum(meta[:, :, 2 * pairs :], axis=(0, 1)) * (
        experts / (rows * devices * top)
    )
    mine = me * owned + lax.iota(jnp.int32, owned)
    before = (lax.iota(jnp.int32, rows)[:, None] < lax.iota(jnp.int32, rows)[None, :]).astype(bf16)

    def apply(half):
        ids_all = meta[half, :, :pairs].reshape(others, rows, top).astype(jnp.int32)
        w_all = meta[half, :, pairs : 2 * pairs].reshape(others, rows, top)
        hit = (ids_all[:, None, :, :] == mine[None, :, None, None]).astype(f32)
        chosen = jnp.sum(hit, axis=3)
        share = jnp.sum(hit * w_all[:, None, :, :], axis=3)
        slot = jnp.einsum("bet,tu->beu", chosen.astype(bf16), before, preferred_element_type=f32)
        slot = jnp.where(chosen > 0, slot, -1.0)
        pick = slot[:, :, None, :] == lax.iota(jnp.int32, CAP).astype(f32)[None, None, :, None]
        scale = jnp.sum(jnp.where(pick, share[:, :, None, :], 0.0), axis=3)
        pick = pick.astype(bf16)
        gate = up = 0.0
        for p in range(3):
            x = jnp.einsum("best,btd->ebsd", pick, arrived[half][p], preferred_element_type=f32)
            x = x.astype(bf16).reshape(owned, others * CAP, -1)
            gate += jnp.einsum(
                "ekd,efd->ekf", x, gate_weight[:, :, spans[p]], preferred_element_type=f32
            )
            up += jnp.einsum(
                "ekd,efd->ekf", x, up_weight[:, :, spans[p]], preferred_element_type=f32
            )
        hidden = (jax.nn.silu(gate) * up).astype(bf16)
        scale = scale.transpose(1, 0, 2).reshape(owned, others * CAP, 1)
        return pick, hidden, scale

    def finish(half, p, after=None):
        pick, hidden, scale = half
        if after is not None:
            probe = after.reshape(-1)[0].astype(f32)
            scale = jnp.where(probe != probe, probe, scale)
        y = jnp.einsum(
            "ekf,efd->ekd", hidden, down_weight[:, :, spans[p]], preferred_element_type=f32
        )
        y = (y * scale).astype(bf16).reshape(owned, others, CAP, -1)
        part = jnp.einsum("best,ebsd->btd", pick, y, preferred_element_type=f32)
        return part.astype(bf16).reshape((2,) * depth + (rows, -1))

    keep, give = apply(0), apply(1)
    mixed = [None] * 3
    kept = total = None
    for p in (1, 0, 2):
        theirs = swap(finish(give, p, kept), pair)
        kept = finish(keep, p, total)
        total = (kept.astype(f32) + theirs.astype(f32)).astype(bf16)
        mixed[p] = collect(total, orders[p])
    return jnp.concatenate(mixed, axis=1), expert_load


def solution(mesh):
    in_specs = (
        P(AXES, None),
        P(AXES, None),
        P(AXES, None),
        P(AXES, None, None),
        P(AXES, None, None),
        P(AXES, None, None),
    )
    return jax.shard_map(
        on_device, mesh=mesh, in_specs=in_specs, out_specs=(P(AXES, None), P()), check_vma=False
    )
```
